128 devices in a mesh: frame: 8 (over y, core), tile: 16 (over x, z).
Axes of the slice: x: 4, y: 4, z: 4, core: 2. Of those that a mesh axis runs over, the one named last changes fastest.
Arguments:
- movie: bfloat16 [64, 2, 1024, 2048], P('frame', None, 'tile'), may hold values from -6 to 6
- shifts: int32 [64, 2], P('frame'), may hold values from -8 to 8, as said below
- filters: float32 [2, 64], replicated, may hold values from -0.5 to 0.5
- weights: bfloat16 [16384, 32768], P(('frame', 'tile')), may hold values from -0.03125 to 0.03125
- slot_owner: int32 [16384, 1], P(('frame', 'tile')), may hold values from 0 to 127; in each aligned block of 128 rows (0 to 127, 128 to 255, ...) at most 2 rows name the same one
- slot_local: int32 [16384, 1], P(('frame', 'tile')), may hold values from 0 to 31
Outputs:
- traces: float32 [4096, 64], P(('frame', 'tile'))
The draws below stay inside these ranges and needn't reach their ends.
Inputs may be any that keep to these rules, and one draw needn't show every extreme that they name: `shifts`: each offset has magnitude at most 8; a row offset of 8 and one of -8 occur in every draw. `slot_owner`: among the 128 entries of one pixel tile no owner is named more than 2 times.
All inputs are finite; a program needn't handle non-finite values.
Results may differ from the reference program's by a relative error of at most 0.0047.
Values may be sent and summed in bfloat16 or wider, within the bound.
A program may use at most 128 MiB of HBM per device.

```python
import math
import jax
import jax.numpy as jnp
import numpy as np
from jax import lax

CB = 16
COMP_DEV = 32
TAPS = 64
MAXS = 8
RAD = 3
CAP = 2
FRAMES = 64
HEIGHT = 1024
WIDTH = 2048
PIXT = 32768
SLOTS = 128
ENTRIES = 16384
COMPONENTS = 4096
DEVICES = 128


def draw_shifts(key, part):
    values = jax.random.randint(key, (FRAMES, 2), -MAXS, MAXS + 1)
    first = jax.random.randint(jax.random.fold_in(key, 1), (), 0, FRAMES)
    second = (first + FRAMES // 2) % FRAMES
    values = values.at[first, 0].set(MAXS)
    values = values.at[second, 0].set(-MAXS)
    return values.astype(jnp.int32)


def set_ends(entries, key, least, largest):
    shape = entries.shape
    place = [jax.random.randint(jax.random.fold_in(key, axis), (), 0, shape[axis]) for axis in range(len(shape))]
    entries = entries.at[tuple(place)].set(least)
    longest = shape.index(max(shape))
    place[longest] = (place[longest] + 1) % shape[longest]
    return entries.at[tuple(place)].set(largest)


def levels(stream_key, extent, shards, low, largest):
    level, own = 1.0, jax.random.fold_in(stream_key, 6)
    for position, shards_of in shards:
        draws = jnp.exp(jax.random.uniform(jax.random.fold_in(own, position), (shards_of,), jnp.float32, low / len(shards), largest / len(shards)))
        level = level * jnp.repeat(draws, extent[position] // shards_of).reshape([-1 if axis == position else 1 for axis in range(len(extent))])
    return level


def routed_block(own_key, own, number, rows, amount, top, bound, slope):
    sequence = jax.random.permutation(own_key, amount)
    heavy_load, usual = load_shares(amount, rows * top, bound, slope, True), load_shares(amount, rows * top, bound, slope, False)
    places = jnp.arange(amount)

    def named(tallies, offset_by):
        used = int((tallies > 0).sum())
        fixed = max(1, used // 4)
        moved = fixed + (places - fixed + offset_by * (used - fixed)) % max(1, amount - fixed)
        return jnp.zeros((amount,), jnp.int32).at[sequence[jnp.where(places < fixed, places, moved)]].set(jnp.asarray(tallies, jnp.int32))

    tallies = jnp.where(number % 4 == 0, named(heavy_load, number // 4), named(usual, number - number // 4 - 1))
    mixed = jax.random.permutation(jax.random.fold_in(own, 3), amount)
    source_of, sink = mixed[0:amount // 2 * 2:2], mixed[1:amount // 2 * 2:2]
    slack = jnp.minimum(tallies[source_of] - 1, bound - tallies[sink]) // 2
    slack = jnp.where((source_of == sequence[0]) | (sink == sequence[0]) | (tallies[sink] == 0), 0, jnp.maximum(slack, 0))
    moved = jax.random.randint(jax.random.fold_in(own, 4), (amount // 2,), 0, 1 << 20) % (slack + 1)
    tallies = tallies.at[source_of].add(-moved).at[sink].add(moved)
    members = jnp.searchsorted(jnp.cumsum(tallies), jnp.arange(rows * top), side="right").astype(jnp.int32)
    grid = members.reshape(top, rows).T
    grid = grid[jax.random.permutation(jax.random.fold_in(own, 1), rows)]
    offset_by = jax.random.randint(jax.random.fold_in(own, 2), (rows, 1), 0, top)
    return jnp.take_along_axis(grid, (jnp.arange(top)[None, :] + offset_by) % top, axis=1)


def load_shares(count, total, bound, lean, full):
    weights = [(1 << 20) // math.isqrt(grade ** lean) + 1 for grade in range(1, count + 1)]
    largest = bound if full else min(bound, max(-(-total // count), total * weights[0] // sum(weights)))
    least = 1 if total - largest >= count - 1 else 0
    given, rest = [largest] + [least] * (count - 1), total - largest - least * (count - 1)
    while rest > 0:
        free = [i for i in range(1, count) if given[i] < largest] or [i for i in range(1, count) if given[i] < bound]
        mass, remaining = sum([weights[i] for i in free]), rest
        for i in free:
            more = min(bound - given[i], max(1, remaining * weights[i] // mass), rest)
            given[i] = given[i] + more
            rest = rest - more
    return np.array(given)


def gaussian(stream_key, shape, scale, most, shards=(), kind=jnp.bfloat16):
    level = levels(stream_key, shape, shards, -0.22, 0.18) if shards else 1.0
    values = jax.random.normal(stream_key, shape, jnp.float32) * scale * level
    return jnp.minimum(jnp.maximum(values, -most), most).astype(kind)


def setup_inputs(seed: int = 0) -> dict:
    arg_keys = jax.random.split(jax.random.key(seed), 7)
    movie = gaussian(arg_keys[0], (FRAMES, 2, HEIGHT, WIDTH), 1.0, 6.0, ((0, 8), (2, 16)))
    shifts = draw_shifts(jax.random.fold_in(arg_keys[6], 71), 0)
    filters = jnp.clip(jax.random.uniform(arg_keys[2], (2, TAPS), jnp.float32, -0.5, 0.5), -0.5, 0.5)
    weights = gaussian(arg_keys[3], (ENTRIES, PIXT), PIXT ** -0.5, 0.03125, ((0, 128),))
    slot_owner_keys = jax.random.split(jax.random.fold_in(arg_keys[4], 1), ENTRIES // SLOTS)
    slot_owner_turns = jax.random.permutation(jax.random.fold_in(arg_keys[4], 3), ENTRIES // SLOTS)
    slot_owner = jax.vmap(lambda own, number: routed_block(jax.random.fold_in(arg_keys[4], 2), own, number, SLOTS, DEVICES, 1, CAP, 1))(slot_owner_keys, slot_owner_turns).reshape((ENTRIES, 1))
    slot_local = set_ends(jax.random.randint(arg_keys[5], (ENTRIES, 1), 0, COMP_DEV), jax.random.fold_in(arg_keys[5], 1), 0, COMP_DEV - 1).astype(jnp.int32)
    return {"movie": movie, "shifts": shifts, "filters": filters, "weights": weights, "slot_owner": slot_owner, "slot_local": slot_local}


smooth_sigma = 1.0


def gauss_taps():
    positions = jnp.arange(-RAD, RAD + 1).astype(jnp.float32)
    values = jnp.exp(-positions * positions / (2.0 * smooth_sigma * smooth_sigma))
    return values / jnp.sum(values)


def build_kernel(filters, count):
    later = jnp.arange(count)[:, None]
    earlier = jnp.arange(count)[None, :]
    offsets = later - earlier
    onehot = (offsets[:, :, None] == jnp.arange(TAPS)[None, None, :]).astype(jnp.float32)
    return jnp.sum(onehot[None] * filters[:, None, None, :].astype(jnp.float32), axis=-1).astype(jnp.bfloat16)


def smooth_frame(frame_data, offset):
    padded = jnp.pad(frame_data, ((0, 0), (MAXS, MAXS), (MAXS, MAXS)))
    starts = (jnp.int32(0), (MAXS - offset[0]).astype(jnp.int32), (MAXS - offset[1]).astype(jnp.int32))
    registered = lax.dynamic_slice(padded, starts, (2, HEIGHT, WIDTH)).astype(jnp.float32)
    wide = jnp.pad(registered, ((0, 0), (RAD, RAD), (RAD, RAD)))
    taps = gauss_taps()
    vertical = taps[0] * wide[:, 0:HEIGHT, :]
    for tap_index in range(1, 2 * RAD + 1):
        vertical = vertical + taps[tap_index] * wide[:, tap_index:tap_index + HEIGHT, :]
    smoothed = taps[0] * vertical[:, :, 0:WIDTH]
    for tap_index in range(1, 2 * RAD + 1):
        smoothed = smoothed + taps[tap_index] * vertical[:, :, tap_index:tap_index + WIDTH]
    return smoothed.astype(jnp.bfloat16)


def reference(movie, shifts, filters, weights, slot_owner, slot_local):
    smoothed = lax.map(lambda pair: smooth_frame(pair[0], pair[1]), (movie, shifts))
    kernel = build_kernel(filters, FRAMES)

    def per_tile(tile_number):
        start = (tile_number * CB).astype(jnp.int32)
        columns = lax.dynamic_slice_in_dim(smoothed, start, CB, 3).reshape(FRAMES, 2, HEIGHT * CB)
        planes_out = [jnp.dot(kernel[plane], columns[:, plane, :], preferred_element_type=jnp.float32) for plane in range(2)]
        filtered = jnp.stack(planes_out, axis=1)
        spikes = jnp.maximum(filtered, 0.0).astype(jnp.bfloat16).reshape(FRAMES, PIXT)
        tile_weights = lax.dynamic_slice_in_dim(weights, (tile_number * SLOTS).astype(jnp.int32), SLOTS, 0)
        return jnp.dot(tile_weights, spikes.T, preferred_element_type=jnp.float32)

    partial_value = lax.map(per_tile, jnp.arange(DEVICES).astype(jnp.int32)).reshape(ENTRIES, FRAMES)
    component = (slot_owner[:, 0] * COMP_DEV + slot_local[:, 0]).astype(jnp.int32)
    return jax.ops.segment_sum(partial_value, component, num_segments=COMPONENTS)
```

```python
import jax
import jax.numpy as jnp
from jax import lax
from jax.experimental import pallas as pl
from jax.experimental.pallas import tpu as pltpu
from jax.sharding import PartitionSpec as P

COMP_DEV = 32
TAPS = 64
MAXS = 8
RAD = 3
CB = 16
MESH = pl.DeviceIdType.MESH

SCALE = 1.6543
TAP = (0.66015625, 0.400390625, 0.08935546875, 0.00732421875)
UNSCALE = 1.0 / (SCALE * SCALE)

NY, NC, NX, NZ = 4, 2, 4, 4
NF, NT, ND = 8, 16, 128
FR = 8
F = 64
ROWS = 64
W = 2048
PAD = 128
HIGHEST = lax.Precision.HIGHEST

PHASES = (((1, 1), (3, 1)), ((1, 0), (3, 0)), ((0, 1), (2, 1)), ((2, 0), (0, 0)))
INNER = ((2, 2), (1, 2), (2, 3), (3, 1), (2, 1), (3, 2), (1, 3), (1, 1),
         (3, 3), (0, 2), (2, 0), (1, 0), (0, 3), (3, 0), (0, 1), (0, 0))


def taps_of(distance):
    d = jnp.abs(distance)
    out = jnp.where(d == 3, TAP[3], 0.0)
    out = jnp.where(d == 2, TAP[2], out)
    out = jnp.where(d == 1, TAP[1], out)
    return jnp.where(d == 0, TAP[0], out)


def iota(shape, dim):
    return lax.broadcasted_iota(jnp.int32, shape, dim)


def kernel(shifts, filters, movie, weights, owner, local, out,
           mbuf, smat, send, recv, shsend, shrecv, wload, tr, wt, vmat, vbuf, kmat, sel,
           idsend, idrecv, fsend, frecv,
           load_sem, own_sem, send_sem, recv_sem, sh_sem, id_sem, f_sem):
    frame = lax.axis_index("frame")
    tile = lax.axis_index("tile")
    y, core, x, z = frame // NC, frame % NC, tile // NZ, tile % NZ
    me = frame * NT + tile

    load_movie = pltpu.make_async_copy(movie, mbuf.at[:, :, :, pl.ds(PAD, W)], load_sem.at[0])
    load_movie.start()
    barrier = pltpu.get_barrier_semaphore()

    def greet(i, _):
        q = (me + i) % ND
        pl.semaphore_signal(barrier, inc=1, device_id=(q // NT, q % NT), device_id_type=MESH)
        return 0

    lax.fori_loop(1, ND, greet, 0)

    across = iota((CB * NT, 512), 1) - PAD - iota((CB * NT, 512), 0)
    for f in range(FR):
        smat[f] = taps_of(across + shifts[f, 1]).astype(jnp.bfloat16)
        shsend[f] = jnp.full((1, 128), shifts[f, 0], jnp.int32).astype(jnp.float32)
    mbuf[:, :, :, 0:PAD] = jnp.zeros((FR, 2, ROWS, PAD), jnp.bfloat16)
    mbuf[:, :, :, PAD + W:] = jnp.zeros((FR, 2, ROWS, PAD), jnp.bfloat16)
    recv[:, 0] = jnp.zeros((NF, FR, CB, 128), jnp.bfloat16)
    recv[:, NT + 1] = jnp.zeros((NF, FR, CB, 128), jnp.bfloat16)
    shrecv[frame] = shsend[...]
    load_movie.wait()
    load_weights = pltpu.make_async_copy(weights, wload, load_sem.at[1])
    load_weights.start()
    lane = iota((2, ROWS, PAD), 2)
    for f in range(FR):
        s = shifts[f, 1]
        first = mbuf[f, :, :, PAD:2 * PAD].astype(jnp.float32)
        mbuf[f, :, :, PAD:2 * PAD] = jnp.where(lane + s >= 0, first, 0.0).astype(jnp.bfloat16)
        last = mbuf[f, :, :, W:W + PAD].astype(jnp.float32)
        mbuf[f, :, :, W:W + PAD] = jnp.where(lane + s < PAD, last, 0.0).astype(jnp.bfloat16)

    def block_of(dy, dc):
        return (y + dy) % NY * NC + (core + dc) % NC

    def smooth_block(dy, dc):
        block = block_of(dy, dc)

        def one(f, _):
            window = mbuf[f, :, :, pl.ds(pl.multiple_of(block * CB * NT, CB * NT), 512)]
            res = lax.dot_general(smat[f], window.reshape(2 * ROWS, 512), (((1,), (1,)), ((), ())),
                                  preferred_element_type=jnp.float32)
            send[pl.ds(block * NT, NT), f] = res.astype(jnp.bfloat16).reshape(NT, CB, 2 * ROWS)
            return 0

        lax.fori_loop(0, FR, one, 0, unroll=2)

    def piece(phase, dy, dc, dx, dz):
        b = block_of(dy, dc)
        t = (x + dx) % NX * NZ + (z + dz) % NZ
        return pltpu.make_async_remote_copy(
            src_ref=send.at[b * NT + t], dst_ref=recv.at[frame, tile + 1],
            send_sem=send_sem.at[phase], recv_sem=recv_sem.at[phase],
            device_id=(b, t), device_id_type=MESH)

    own = pltpu.make_async_copy(send.at[me], recv.at[frame, tile + 1], own_sem.at[0])
    for phase, pair in enumerate(PHASES):
        for dy, dc in pair:
            smooth_block(dy, dc)
        if phase == 0:
            pl.semaphore_wait(barrier, ND - 1)
            for k in range(1, NF):
                pltpu.make_async_remote_copy(
                    src_ref=shsend, dst_ref=shrecv.at[frame], send_sem=sh_sem.at[0],
                    recv_sem=sh_sem.at[1], device_id=((frame + k) % NF, tile),
                    device_id_type=MESH).start()
        for dx, dz in INNER:
            for sign, (dy, dc) in zip((1, -1), pair):
                ex, ez = (sign * dx) % NX, (sign * dz) % NZ
                if (dy, dc, ex, ez) == (0, 0, 0, 0):
                    own.start()
                else:
                    piece(phase, dy, dc, ex, ez).start()

    owns = (owner[...] == iota((128, ND), 1)).astype(jnp.float32)
    before = (iota((128, 128), 1) < iota((128, 128), 0)).astype(jnp.bfloat16)
    count = jnp.dot(before, owns.astype(jnp.bfloat16), preferred_element_type=jnp.float32)
    ids = local[...].astype(jnp.float32)
    names = []
    for slot in range(2):
        taken = jnp.where(count == float(slot), owns, 0.0)
        sel[slot] = taken
        names.append(jnp.broadcast_to(jnp.sum(taken * ids, axis=0, keepdims=True), (64, ND)))
    idsend[...] = jnp.concatenate(names, axis=0).T.reshape(ND, 1, 128)

    def send_ids(i, _):
        q = (me + i) % ND
        pltpu.make_async_remote_copy(
            src_ref=idsend.at[q], dst_ref=idrecv.at[me], send_sem=id_sem.at[0],
            recv_sem=id_sem.at[1], device_id=(q // NT, q % NT), device_id_type=MESH).start()
        return 0

    lax.fori_loop(1, ND, send_ids, 0)
    own_id = pltpu.make_async_copy(idsend.at[me], idrecv.at[me], own_sem.at[1])
    own_id.start()

    offset = iota((F, F), 0) - iota((F, F), 1)
    for p in range(2):
        def put(i, acc):
            return jnp.where(offset == i, filters[p, i], acc)
        kmat[p] = lax.fori_loop(0, TAPS, put, jnp.zeros((F, F), jnp.float32)).astype(jnp.bfloat16)

    load_weights.wait()

    def turn(i, _):
        p, j = i // 8, i % 8
        base = pl.multiple_of(i * 2048, 2048)
        for part in range(16):
            piece_w = wload[:, pl.ds(base + part * 128, 128)]
            tr[pl.ds(part * 128, 128), :] = piece_w.astype(jnp.float32).T
        for col in range(CB):
            got = tr[pl.ds(col, 128, stride=CB), :]
            wt[j * CB + col, pl.ds(pl.multiple_of(p * 128, 128), 128), :] = got.astype(jnp.bfloat16)
        return 0

    for slot in range(2):
        vmat[slot] = jnp.zeros((512, 256), jnp.bfloat16)
    distance = iota((256, 128), 0) - 64 - iota((256, 128), 1)
    row = iota((CB, 128), 1) % ROWS

    def vertical(source):
        for f in range(FR):
            shift = shrecv[source, f].astype(jnp.int32)
            band = taps_of(distance + shift).astype(jnp.bfloat16)
            at = f % 2
            for b in range(4):
                part = band[b * 64:(b + 1) * 64]
                vmat[at, b * 128:b * 128 + 64, 0:128] = part
                vmat[at, b * 128 + 64:b * 128 + 128, 128:256] = part
            groups = []
            for b in range(4):
                tiles = []
                for j in range(8):
                    cell = recv[source, 2 * j + b, f]
                    if 2 * j + b == 1:
                        cell = jnp.where(row + shift >= 0, cell.astype(jnp.float32), 0.0).astype(jnp.bfloat16)
                    if 2 * j + b == NT:
                        cell = jnp.where(row + shift < ROWS, cell.astype(jnp.float32), 0.0).astype(jnp.bfloat16)
                    tiles.append(cell)
                groups.append(jnp.concatenate(tiles, axis=0))
            lhs = jnp.concatenate(groups, axis=1)
            res = jnp.dot(lhs, vmat[at], preferred_element_type=jnp.float32) * UNSCALE
            for p in range(2):
                vbuf[p, pl.ds(source * FR + f, 128, stride=F), :] = res[:, p * 128:(p + 1) * 128]

    lax.fori_loop(0, 16, turn, 0)
    pltpu.make_async_copy(shrecv.at[pl.ds(0, NF - 1)], shrecv.at[pl.ds(0, NF - 1)], sh_sem.at[1]).wait()
    for phase, pair in enumerate(PHASES):
        n = 31 if phase == 3 else 32
        pltpu.make_async_copy(send.at[pl.ds(0, n)], send.at[pl.ds(0, n)], recv_sem.at[phase]).wait()
        if phase == 3:
            own.wait()
        for dy, dc in pair:
            vertical(block_of(-dy, -dc))

    def pool(i, acc):
        cells = [jnp.concatenate([vbuf[p, pl.ds(pl.multiple_of((2 * i + h) * F, F), F), :].astype(jnp.bfloat16)
                                  for h in range(2)], axis=1) for p in range(2)]
        spikes = [jnp.maximum(jnp.dot(kmat[p], cells[p], preferred_element_type=jnp.float32), 0.0).astype(jnp.bfloat16)
                  for p in range(2)]
        for h in range(2):
            both = jnp.concatenate([spikes[p][:, h * 128:(h + 1) * 128] for p in range(2)], axis=1)
            acc = acc + jnp.dot(both, wt[2 * i + h], preferred_element_type=jnp.float32)
        return acc

    acc = lax.fori_loop(0, 64, pool, jnp.zeros((F, 128), jnp.float32), unroll=2)

    slots = [jnp.dot(acc, sel[slot], preferred_element_type=jnp.float32, precision=HIGHEST) for slot in range(2)]
    fsend[...] = jnp.concatenate(slots, axis=0).T.reshape(ND, 1, 128)
    for dx, dz in INNER:
        for pair in PHASES:
            for sign, (dy, dc) in zip((1, -1), pair):
                ex, ez = (sign * dx) % NX, (sign * dz) % NZ
                if (dy, dc, ex, ez) == (0, 0, 0, 0):
                    continue
                b = block_of(dy, dc)
                t = (x + ex) % NX * NZ + (z + ez) % NZ
                pltpu.make_async_remote_copy(
                    src_ref=fsend.at[b * NT + t], dst_ref=frecv.at[me], send_sem=f_sem.at[0],
                    recv_sem=f_sem.at[1], device_id=(b, t), device_id_type=MESH).start()
    own_f = pltpu.make_async_copy(fsend.at[me], frecv.at[me], own_sem.at[2])
    own_f.start()

    for phase in range(4):
        n = 31 if phase == 3 else 32
        pltpu.make_async_copy(send.at[pl.ds(0, n)], send.at[pl.ds(0, n)], send_sem.at[phase]).wait()
    pltpu.make_async_copy(shrecv.at[pl.ds(0, NF - 1)], shrecv.at[pl.ds(0, NF - 1)], sh_sem.at[0]).wait()
    for k in range(2):
        pltpu.make_async_copy(idsend.at[pl.ds(0, ND - 1)], idsend.at[pl.ds(0, ND - 1)], id_sem.at[k]).wait()
    own_id.wait()
    got = idrecv[...].reshape(ND, 128)
    component = iota((ND, COMP_DEV), 1).astype(jnp.float32)
    hot = jnp.concatenate([(got[:, 0:COMP_DEV] == component).astype(jnp.float32),
                           (got[:, 64:64 + COMP_DEV] == component).astype(jnp.float32)], axis=1).T
    pltpu.make_async_copy(fsend.at[pl.ds(0, ND - 1)], fsend.at[pl.ds(0, ND - 1)], f_sem.at[1]).wait()
    own_f.wait()
    total = jnp.dot(hot, frecv[...].reshape(ND, 128), preferred_element_type=jnp.float32, precision=HIGHEST)
    out[...] = total[0:COMP_DEV, 0:F] + total[COMP_DEV:, F:2 * F]
    pltpu.make_async_copy(fsend.at[pl.ds(0, ND - 1)], fsend.at[pl.ds(0, ND - 1)], f_sem.at[0]).wait()


def body(movie, shifts, filters, weights, slot_owner, slot_local):
    bf16, f32 = jnp.bfloat16, jnp.float32
    vmem = pl.BlockSpec(memory_space=pltpu.VMEM)
    smem = pl.BlockSpec(memory_space=pltpu.SMEM)
    anywhere = pl.BlockSpec(memory_space=pl.ANY)
    dma = pltpu.SemaphoreType.DMA
    return pl.pallas_call(
        kernel,
        out_shape=jax.ShapeDtypeStruct((COMP_DEV, F), f32),
        in_specs=[smem, smem, anywhere, anywhere, vmem, vmem],
        out_specs=vmem,
        scratch_shapes=[
            pltpu.VMEM((FR, 2, ROWS, W + 2 * PAD), bf16),
            pltpu.VMEM((FR, CB * NT, 512), bf16),
            pltpu.VMEM((ND, FR, CB, 128), bf16),
            pltpu.VMEM((NF, NT + 2, FR, CB, 128), bf16),
            pltpu.VMEM((FR, 1, 128), f32),
            pltpu.VMEM((NF, FR, 1, 128), f32),
            pltpu.VMEM((128, 32768), bf16),
            pltpu.VMEM((2048, 128), f32),
            pltpu.VMEM((128, 256, 128), bf16),
            pltpu.VMEM((2, 512, 256), bf16),
            pltpu.VMEM((2, 128 * F, 128), f32),
            pltpu.VMEM((2, F, F), bf16),
            pltpu.VMEM((2, 128, ND), f32),
            pltpu.VMEM((ND, 1, 128), f32),
            pltpu.VMEM((ND, 1, 128), f32),
            pltpu.VMEM((ND, 1, 128), f32),
            pltpu.VMEM((ND, 1, 128), f32),
            dma((2,)), dma((3,)), dma((4,)), dma((4,)), dma((2,)), dma((2,)), dma((2,)),
        ],
        compiler_params=pltpu.CompilerParams(
            collective_id=0, has_side_effects=True, vmem_limit_bytes=60 * 1024 * 1024),
        cost_estimate=pl.CostEstimate(flops=8_000_000_000, bytes_accessed=24_000_000, transcendentals=0),
    )(shifts, filters, movie, weights, slot_owner, slot_local)


def solution(mesh):
    in_specs = (
        P("frame", None, "tile", None),
        P("frame", None),
        P(),
        P(("frame", "tile"), None),
        P(("frame", "tile"), None),
        P(("frame", "tile"), None),
    )
    out_specs = P(("frame", "tile"), None)
    return jax.shard_map(body, mesh=mesh, in_specs=in_specs, out_specs=out_specs, check_vma=False)
```

```python
import jax
import jax.numpy as jnp
from jax import lax
from jax.experimental import pallas as pl
from jax.experimental.pallas import tpu as pltpu
from jax.sharding import PartitionSpec as P

COMP_DEV = 32
TAPS = 64
MAXS = 8
RAD = 3
CB = 16
MESH = pl.DeviceIdType.MESH

SCALE = 1.6543
TAP = (0.66015625, 0.400390625, 0.08935546875, 0.00732421875)
UNSCALE = 1.0 / (SCALE * SCALE)

NY, NC, NX, NZ = 4, 2, 4, 4
NF, NT, ND = 8, 16, 128
FR = 8
F = 64
ROWS = 64
W = 2048
PAD = 128
HIGHEST = lax.Precision.HIGHEST

PHASES = (((1, 1), (3, 1)), ((1, 0), (3, 0)), ((0, 1), (2, 1)), ((2, 0), (0, 0)))
NP = len(PHASES)
INNER = tuple((a, (a + b) % 4) for b in (2, 1, 3, 0) for a in (2, 1, 3, 0))
HC = CB // 2
FP = FR // 2


def taps_of(distance):
    d = jnp.abs(distance)
    out = jnp.where(d == 3, TAP[3], 0.0)
    out = jnp.where(d == 2, TAP[2], out)
    out = jnp.where(d == 1, TAP[1], out)
    return jnp.where(d == 0, TAP[0], out)


def iota(shape, dim):
    return lax.broadcasted_iota(jnp.int32, shape, dim)


def kernel(shifts, filters, movie, weights, owner, local, out,
           mbuf, smat, send, recv, shsend, shrecv, wload, tr, wt, bands, vbuf, kmat, sel,
           idsend, idrecv, fsend, frecv,
           load_sem, own_sem, send_sem, recv_sem, sh_sem, id_sem, f_sem):
    frame = lax.axis_index("frame")
    tile = lax.axis_index("tile")
    y, core, x, z = frame // NC, frame % NC, tile // NZ, tile % NZ
    me = frame * NT + tile

    load_movie = pltpu.make_async_copy(movie, mbuf.at[:, :, :, pl.ds(PAD, W)], load_sem.at[0])
    load_movie.start()
    barrier = pltpu.get_barrier_semaphore()

    def greet(i, _):
        q = (me + i) % ND
        pl.semaphore_signal(barrier, inc=1, device_id=(q // NT, q % NT), device_id_type=MESH)
        return 0

    lax.fori_loop(1, ND, greet, 0)

    line = iota((128, 384), 0)
    place = line % 64 // HC * CB + line // 64 * HC + line % HC
    across = iota((128, 384), 1) - PAD - place
    for f in range(FR):
        stencil = taps_of(across + shifts[f, 1]).astype(jnp.bfloat16)
        for h in range(2):
            for a in range(2):
                r = h * 128 + a * 64
                smat[f, r:r + 64, a * 128:a * 128 + 384] = stencil[h * 64:h * 64 + 64]
                blank = 384 - a * 384
                smat[f, r:r + 64, blank:blank + 128] = jnp.zeros((64, 128), jnp.bfloat16)
        shsend[f] = jnp.full((1, 128), shifts[f, 0], jnp.int32).astype(jnp.float32)
    mbuf[:, :, :, 0:PAD] = jnp.zeros((FR, 2, ROWS, PAD), jnp.bfloat16)
    mbuf[:, :, :, PAD + W:] = jnp.zeros((FR, 2, ROWS, PAD), jnp.bfloat16)
    load_movie.wait()
    load_weights = pltpu.make_async_copy(weights, wload, load_sem.at[1])
    load_weights.start()
    lane = iota((2, ROWS, PAD), 2)
    for f in range(FR):
        s = shifts[f, 1]
        first = mbuf[f, :, :, PAD:2 * PAD].astype(jnp.float32)
        mbuf[f, :, :, PAD:2 * PAD] = jnp.where(lane + s >= 0, first, 0.0).astype(jnp.bfloat16)
        last = mbuf[f, :, :, W:W + PAD].astype(jnp.float32)
        mbuf[f, :, :, W:W + PAD] = jnp.where(lane + s < PAD, last, 0.0).astype(jnp.bfloat16)

    def block_of(dy, dc):
        return (y + dy) % NY * NC + (core + dc) % NC

    def smooth_block(dy, dc):
        block = block_of(dy, dc)

        def one(fp, _):
            res = []
            for q in range(2):
                f = 2 * fp + q
                window = mbuf[f, :, :, pl.ds(pl.multiple_of(block * CB * NT, CB * NT), 512)]
                cols = lax.dot_general(smat[f], window.reshape(2 * ROWS, 512), (((1,), (1,)), ((), ())),
                                       preferred_element_type=jnp.float32)
                res.append(cols.reshape(2 * NT, HC, 128))
            both = jnp.concatenate(res, axis=1).astype(jnp.bfloat16)
            for h in range(2):
                send[h, pl.ds(block * NT, NT), fp] = both[h * NT:(h + 1) * NT]
            return 0

        lax.fori_loop(0, FP, one, 0, unroll=2)

    def piece(h, phase, dy, dc, dx, dz):
        b = block_of(dy, dc)
        t = (x + dx) % NX * NZ + (z + dz) % NZ
        return pltpu.make_async_remote_copy(
            src_ref=send.at[h, b * NT + t], dst_ref=recv.at[h, frame, tile + 1],
            send_sem=send_sem.at[h * NP + phase], recv_sem=recv_sem.at[h * NP + phase],
            device_id=(b, t), device_id_type=MESH)

    own = [pltpu.make_async_copy(send.at[h, me], recv.at[h, frame, tile + 1], own_sem.at[h]) for h in range(2)]
    for h in range(2):
        for phase, pair in enumerate(PHASES):
            if h == 0:
                for dy, dc in pair:
                    smooth_block(dy, dc)
            if h == 0 and phase == 0:
                pl.semaphore_wait(barrier, ND - 1)
                for k in range(1, NF):
                    pltpu.make_async_remote_copy(
                        src_ref=shsend, dst_ref=shrecv.at[frame], send_sem=sh_sem.at[0],
                        recv_sem=sh_sem.at[1], device_id=((frame + k) % NF, tile),
                        device_id_type=MESH).start()
            for dx, dz in INNER:
                for sign, (dy, dc) in zip((1, -1), pair):
                    ex, ez = (sign * dx) % NX, (sign * dz) % NZ
                    if (dy, dc, ex, ez) == (0, 0, 0, 0):
                        own[h].start()
                    else:
                        piece(h, phase, dy, dc, ex, ez).start()

    shrecv[frame] = shsend[...]
    for h in range(2):
        recv[h, :, 0] = jnp.zeros((NF, FP, CB, 128), jnp.bfloat16)
        recv[h, :, NT + 1] = jnp.zeros((NF, FP, CB, 128), jnp.bfloat16)

    owns = (owner[...] == iota((128, ND), 1)).astype(jnp.float32)
    before = (iota((128, 128), 1) < iota((128, 128), 0)).astype(jnp.bfloat16)
    count = jnp.dot(before, owns.astype(jnp.bfloat16), preferred_element_type=jnp.float32)
    ids = local[...].astype(jnp.float32)
    names = []
    for slot in range(2):
        taken = jnp.where(count == float(slot), owns, 0.0)
        sel[slot] = taken
        names.append(jnp.broadcast_to(jnp.sum(taken * ids, axis=0, keepdims=True), (64, ND)))
    idsend[...] = jnp.concatenate(names, axis=0).T.reshape(ND, 1, 128)

    def send_ids(i, _):
        q = (me + i) % ND
        pltpu.make_async_remote_copy(
            src_ref=idsend.at[q], dst_ref=idrecv.at[me], send_sem=id_sem.at[0],
            recv_sem=id_sem.at[1], device_id=(q // NT, q % NT), device_id_type=MESH).start()
        return 0

    lax.fori_loop(1, ND, send_ids, 0)
    own_id = pltpu.make_async_copy(idsend.at[me], idrecv.at[me], own_sem.at[2])
    own_id.start()

    offset = iota((F, F), 0) - iota((F, F), 1)
    for p in range(2):
        def put(i, acc):
            return jnp.where(offset == i, filters[p, i], acc)
        kmat[p] = lax.fori_loop(0, TAPS, put, jnp.zeros((F, F), jnp.float32)).astype(jnp.bfloat16)

    pltpu.make_async_copy(shrecv.at[pl.ds(0, NF - 1)], shrecv.at[pl.ds(0, NF - 1)], sh_sem.at[1]).wait()
    distance = iota((256, 128), 0) - ROWS - iota((256, 128), 1)

    def build(i, _):
        for q in range(2):
            shift = shrecv[i // FP, i % FP * 2 + q].astype(jnp.int32)
            bands[i, :, q * 128:(q + 1) * 128] = taps_of(distance + shift).astype(jnp.bfloat16)
        return 0

    lax.fori_loop(0, NF * FP, build, 0)

    load_weights.wait()

    def turn(i, _):
        p, j = i // 8, i % 8
        base = pl.multiple_of(i * 2048, 2048)
        for part in range(16):
            piece_w = wload[:, pl.ds(base + part * 128, 128)]
            tr[pl.ds(part * 128, 128), :] = piece_w.astype(jnp.float32).T
        for col in range(CB):
            got = tr[pl.ds(col, 128, stride=CB), :]
            wt[col // HC, j, p, pl.ds(col % HC * 128, 128), :] = got.astype(jnp.bfloat16)
        return 0

    lax.fori_loop(0, 16, turn, 0)

    row = iota((CB, 128), 1) % ROWS
    second = iota((CB, 128), 0) >= HC

    def vertical(h, source):
        def one(fp, _):
            shift = jnp.where(second, shrecv[source, 2 * fp + 1], shrecv[source, 2 * fp]).astype(jnp.int32) + row
            groups = []
            for b in range(4):
                tiles = []
                for j in range(8):
                    cell = recv[h, source, 2 * j + b, fp]
                    if 2 * j + b == 1:
                        cell = jnp.where(shift >= 0, cell.astype(jnp.float32), 0.0).astype(jnp.bfloat16)
                    if 2 * j + b == NT:
                        cell = jnp.where(shift < ROWS, cell.astype(jnp.float32), 0.0).astype(jnp.bfloat16)
                    tiles.append(cell)
                groups.append(jnp.concatenate(tiles, axis=0))
            lhs = jnp.concatenate([
                jnp.concatenate([groups[b][:, p * ROWS:(p + 1) * ROWS] for b in range(4)], axis=1)
                for p in range(2)], axis=0)
            res = jnp.dot(lhs, bands[source * FP + fp], preferred_element_type=jnp.float32) * UNSCALE
            res = res.reshape(CB, 2, HC, 256)
            for q in range(2):
                vbuf[pl.ds(source * FR + 2 * fp + q, 128, stride=F), :] = (
                    res[:, q, :, q * 128:(q + 1) * 128].reshape(128, 128))
            return 0

        lax.fori_loop(0, FP, one, 0, unroll=2)

    def pool(h):
        def one(j, acc):
            for p in range(2):
                cells = jnp.concatenate([
                    vbuf[pl.ds(pl.multiple_of(((p * 8 + j) * HC + c) * F, F), F), :].astype(jnp.bfloat16)
                    for c in range(HC)], axis=1)
                spikes = jnp.maximum(jnp.dot(kmat[p], cells, preferred_element_type=jnp.float32), 0.0)
                acc = acc + jnp.dot(spikes.astype(jnp.bfloat16), wt[h, j, p], preferred_element_type=jnp.float32)
            return acc
        return one

    acc = jnp.zeros((F, 128), jnp.float32)
    for h in range(2):
        for phase, pair in enumerate(PHASES):
            n = 31 if phase == NP - 1 else 32
            arrived = send.at[0, pl.ds(0, n)]
            pltpu.make_async_copy(arrived, arrived, recv_sem.at[h * NP + phase]).wait()
            if phase == NP - 1:
                own[h].wait()
            for dy, dc in pair:
                vertical(h, block_of(-dy, -dc))
        acc = lax.fori_loop(0, 8, pool(h), acc, unroll=2)

    slots = [jnp.dot(acc, sel[slot], preferred_element_type=jnp.float32, precision=HIGHEST) for slot in range(2)]
    fsend[...] = jnp.concatenate(slots, axis=0).T.reshape(ND, 1, 128)
    for dx, dz in INNER:
        for pair in PHASES:
            for sign, (dy, dc) in zip((1, -1), pair):
                ex, ez = (sign * dx) % NX, (sign * dz) % NZ
                if (dy, dc, ex, ez) == (0, 0, 0, 0):
                    continue
                b = block_of(dy, dc)
                t = (x + ex) % NX * NZ + (z + ez) % NZ
                pltpu.make_async_remote_copy(
                    src_ref=fsend.at[b * NT + t], dst_ref=frecv.at[me], send_sem=f_sem.at[0],
                    recv_sem=f_sem.at[1], device_id=(b, t), device_id_type=MESH).start()
    own_f = pltpu.make_async_copy(fsend.at[me], frecv.at[me], own_sem.at[3])
    own_f.start()

    for i in range(2 * NP):
        n = 31 if i % NP == NP - 1 else 32
        left = send.at[0, pl.ds(0, n)]
        pltpu.make_async_copy(left, left, send_sem.at[i]).wait()
    pltpu.make_async_copy(shrecv.at[pl.ds(0, NF - 1)], shrecv.at[pl.ds(0, NF - 1)], sh_sem.at[0]).wait()
    for k in range(2):
        pltpu.make_async_copy(idsend.at[pl.ds(0, ND - 1)], idsend.at[pl.ds(0, ND - 1)], id_sem.at[k]).wait()
    own_id.wait()
    got = idrecv[...].reshape(ND, 128)
    component = iota((ND, COMP_DEV), 1).astype(jnp.float32)
    hot = jnp.concatenate([(got[:, 0:COMP_DEV] == component).astype(jnp.float32),
                           (got[:, 64:64 + COMP_DEV] == component).astype(jnp.float32)], axis=1).T
    pltpu.make_async_copy(fsend.at[pl.ds(0, ND - 1)], fsend.at[pl.ds(0, ND - 1)], f_sem.at[1]).wait()
    own_f.wait()
    total = jnp.dot(hot, frecv[...].reshape(ND, 128), preferred_element_type=jnp.float32, precision=HIGHEST)
    out[...] = total[0:COMP_DEV, 0:F] + total[COMP_DEV:, F:2 * F]
    pltpu.make_async_copy(fsend.at[pl.ds(0, ND - 1)], fsend.at[pl.ds(0, ND - 1)], f_sem.at[0]).wait()


def body(movie, shifts, filters, weights, slot_owner, slot_local):
    bf16, f32 = jnp.bfloat16, jnp.float32
    vmem = pl.BlockSpec(memory_space=pltpu.VMEM)
    smem = pl.BlockSpec(memory_space=pltpu.SMEM)
    anywhere = pl.BlockSpec(memory_space=pl.ANY)
    dma = pltpu.SemaphoreType.DMA
    return pl.pallas_call(
        kernel,
        out_shape=jax.ShapeDtypeStruct((COMP_DEV, F), f32),
        in_specs=[smem, smem, anywhere, anywhere, vmem, vmem],
        out_specs=vmem,
        scratch_shapes=[
            pltpu.VMEM((FR, 2, ROWS, W + 2 * PAD), bf16),
            pltpu.VMEM((FR, CB * NT, 512), bf16),
            pltpu.VMEM((2, ND, FP, CB, 128), bf16),
            pltpu.VMEM((2, NF, NT + 2, FP, CB, 128), bf16),
            pltpu.VMEM((FR, 1, 128), f32),
            pltpu.VMEM((NF, FR, 1, 128), f32),
            pltpu.VMEM((128, 32768), bf16),
            pltpu.VMEM((2048, 128), f32),
            pltpu.VMEM((2, 8, 2, HC * 128, 128), bf16),
            pltpu.VMEM((NF * FP, 256, 256), bf16),
            pltpu.VMEM((128 * F, 128), f32),
            pltpu.VMEM((2, F, F), bf16),
            pltpu.VMEM((2, 128, ND), f32),
            pltpu.VMEM((ND, 1, 128), f32),
            pltpu.VMEM((ND, 1, 128), f32),
            pltpu.VMEM((ND, 1, 128), f32),
            pltpu.VMEM((ND, 1, 128), f32),
            dma((2,)), dma((4,)), dma((2 * NP,)), dma((2 * NP,)), dma((2,)), dma((2,)), dma((2,)),
        ],
        compiler_params=pltpu.CompilerParams(
            collective_id=0, has_side_effects=True, vmem_limit_bytes=60 * 1024 * 1024),
        cost_estimate=pl.CostEstimate(flops=8_000_000_000, bytes_accessed=24_000_000, transcendentals=0),
    )(shifts, filters, movie, weights, slot_owner, slot_local)


def solution(mesh):
    in_specs = (
        P("frame", None, "tile", None),
        P("frame", None),
        P(),
        P(("frame", "tile"), None),
        P(("frame", "tile"), None),
        P(("frame", "tile"), None),
    )
    out_specs = P(("frame", "tile"), None)
    return jax.shard_map(body, mesh=mesh, in_specs=in_specs, out_specs=out_specs, check_vma=False)
```

```python
import jax
import jax.numpy as jnp
from jax import lax
from jax.experimental import pallas as pl
from jax.experimental.pallas import tpu as pltpu
from jax.sharding import PartitionSpec as P

COMP_DEV = 32
TAPS = 64
MAXS = 8
RAD = 3
CB = 16
MESH = pl.DeviceIdType.MESH

SCALE = 1.6543
TAP = (0.66015625, 0.400390625, 0.08935546875, 0.00732421875)
UNSCALE = 1.0 / (SCALE * SCALE)

NY, NC, NX, NZ = 4, 2, 4, 4
NF, NT, ND, NCHIP = 8, 16, 128, 64
FR = 8
F = 64
ROWS = 64
W = 2048
PAD = 128

PHASES = (((1, 1), (3, 1)), ((1, 0), (3, 0)), ((0, 1), (2, 1)), ((2, 0), (0, 0)))
NP = len(PHASES)
INNER = tuple((a, (a + b) % 4) for b in (2, 1, 3, 0) for a in (2, 1, 3, 0))
HC = CB // 2
FP = FR // 2


def taps_of(distance):
    d = jnp.abs(distance)
    out = jnp.where(d == 3, TAP[3], 0.0)
    out = jnp.where(d == 2, TAP[2], out)
    out = jnp.where(d == 1, TAP[1], out)
    return jnp.where(d == 0, TAP[0], out)


def three(value):
    high = value.astype(jnp.bfloat16)
    rest = value - high.astype(jnp.float32)
    middle = rest.astype(jnp.bfloat16)
    return [high, middle, (rest - middle.astype(jnp.float32)).astype(jnp.bfloat16)]


def iota(shape, dim):
    return lax.broadcasted_iota(jnp.int32, shape, dim)


def kernel(shifts, filters, movie, weights, owner, local, out,
           mbuf, smat, send, recv, shsend, shrecv, wload, tr, wt, bands, vbuf, kmat, sel,
           idsend, idrecv, idsib, hot, fsend, frecv, fsib,
           load_sem, own_sem, send_sem, recv_sem, sh_sem, id_sem, f_sem):
    frame = lax.axis_index("frame")
    tile = lax.axis_index("tile")
    y, core, x, z = frame // NC, frame % NC, tile // NZ, tile % NZ
    me = frame * NT + tile
    chip = y * NT + tile

    load_movie = pltpu.make_async_copy(movie, mbuf.at[:, :, :, pl.ds(PAD, W)], load_sem.at[0])
    load_movie.start()
    barrier = pltpu.get_barrier_semaphore()

    def block_of(dy, dc):
        return (y + dy) % NY * NC + (core + dc) % NC

    def tile_of(dx, dz):
        return (x + dx) % NX * NZ + (z + dz) % NZ

    for dx, dz in INNER:
        for dy in (2, 1, 3, 0):
            for dc in (1, 0):
                if (dy, dc, dx, dz) != (0, 0, 0, 0):
                    pl.semaphore_signal(barrier, inc=1, device_id=(block_of(dy, dc), tile_of(dx, dz)),
                                        device_id_type=MESH)

    line = iota((128, 384), 0)
    place = line % 64 // HC * CB + line // 64 * HC + line % HC
    across = iota((128, 384), 1) - PAD - place
    for f in range(FR):
        stencil = taps_of(across + shifts[1, f]).astype(jnp.bfloat16)
        for h in range(2):
            for a in range(2):
                r = h * 128 + a * 64
                smat[f, r:r + 64, a * 128:a * 128 + 384] = stencil[h * 64:h * 64 + 64]
                blank = 384 - a * 384
                smat[f, r:r + 64, blank:blank + 128] = jnp.zeros((64, 128), jnp.bfloat16)
        shsend[f] = jnp.full((1, 128), shifts[0, f], jnp.int32).astype(jnp.float32)
    mbuf[:, :, :, 0:PAD] = jnp.zeros((FR, 2, ROWS, PAD), jnp.bfloat16)
    mbuf[:, :, :, PAD + W:] = jnp.zeros((FR, 2, ROWS, PAD), jnp.bfloat16)
    load_movie.wait()
    load_weights = pltpu.make_async_copy(weights, wload, load_sem.at[1])
    load_weights.start()
    lane = iota((2, ROWS, PAD), 2)
    for f in range(FR):
        s = shifts[1, f]
        first = mbuf[f, :, :, PAD:2 * PAD].astype(jnp.float32)
        mbuf[f, :, :, PAD:2 * PAD] = jnp.where(lane + s >= 0, first, 0.0).astype(jnp.bfloat16)
        last = mbuf[f, :, :, W:W + PAD].astype(jnp.float32)
        mbuf[f, :, :, W:W + PAD] = jnp.where(lane + s < PAD, last, 0.0).astype(jnp.bfloat16)

    def smooth_block(dy, dc):
        block = block_of(dy, dc)

        def one(fp, _):
            res = []
            for q in range(2):
                f = 2 * fp + q
                window = mbuf[f, :, :, pl.ds(pl.multiple_of(block * CB * NT, CB * NT), 512)]
                cols = lax.dot_general(smat[f], window.reshape(2 * ROWS, 512), (((1,), (1,)), ((), ())),
                                       preferred_element_type=jnp.float32)
                res.append(cols.reshape(2 * NT, HC, 128))
            both = jnp.concatenate(res, axis=1).astype(jnp.bfloat16)
            for h in range(2):
                send[h, pl.ds(block * NT, NT), fp] = both[h * NT:(h + 1) * NT]
            return 0

        lax.fori_loop(0, FP, one, 0, unroll=2)

    def piece(h, phase, dy, dc, dx, dz):
        b, t = block_of(dy, dc), tile_of(dx, dz)
        return pltpu.make_async_remote_copy(
            src_ref=send.at[h, b * NT + t], dst_ref=recv.at[h, frame, tile + 1],
            send_sem=send_sem.at[h * NP + phase], recv_sem=recv_sem.at[h * NP + phase],
            device_id=(b, t), device_id_type=MESH)

    def chips(src, dst, sems):
        for dx, dz in INNER:
            for dy in (2, 1, 3, 0):
                if (dy, dx, dz) != (0, 0, 0):
                    t = tile_of(dx, dz)
                    pltpu.make_async_remote_copy(
                        src_ref=src.at[:, (y + dy) % NY * NT + t], dst_ref=dst.at[:, chip],
                        send_sem=sems.at[0], recv_sem=sems.at[1],
                        device_id=(block_of(dy, 0), t), device_id_type=MESH).start()

    def sibling(src, dst, sems):
        return pltpu.make_async_remote_copy(
            src_ref=src.at[1 - core], dst_ref=dst, send_sem=sems.at[2], recv_sem=sems.at[3],
            device_id=(block_of(0, 1), tile), device_id_type=MESH)

    def all_chips(ref, sem):
        part = ref.at[:, pl.ds(0, NCHIP - 1)]
        return pltpu.make_async_copy(part, part, sem)

    def name_entries():
        line = iota((ND, 128), 0)
        who = (line % NCHIP // NT * NC + line // NCHIP) * NT + line % NT
        owns = (owner[...] == who).astype(jnp.float32)
        before = (iota((128, 128), 0) < iota((128, 128), 1)).astype(jnp.bfloat16)
        count = jnp.dot(owns.astype(jnp.bfloat16), before, preferred_element_type=jnp.float32)
        ids = local[...].astype(jnp.float32)
        names = []
        for slot in range(2):
            taken = jnp.where(count == float(slot), owns, 0.0)
            for k in range(3):
                sel[slot * ND:(slot + 1) * ND, k * 128:(k + 1) * 128] = taken.astype(jnp.bfloat16)
            names.append(jnp.broadcast_to(jnp.sum(taken * ids, axis=1, keepdims=True), (ND, 64)))
        idsend[...] = jnp.concatenate(names, axis=1).reshape(NC, NCHIP, 1, 128)
        chips(idsend, idrecv, id_sem)
        own_id.start()

    own_id = pltpu.make_async_copy(idsend.at[:, chip], idrecv.at[:, chip], own_sem.at[2])
    id_forward = sibling(idrecv, idsib, id_sem)
    forward = sibling(frecv, fsib, f_sem)
    own_f = pltpu.make_async_copy(fsend.at[:, chip], frecv.at[:, chip], own_sem.at[3])

    own = [pltpu.make_async_copy(send.at[h, me], recv.at[h, frame, tile + 1], own_sem.at[h]) for h in range(2)]
    for h in range(2):
        if h == 1:
            name_entries()
        for phase, pair in enumerate(PHASES):
            if h == 0:
                for dy, dc in pair:
                    smooth_block(dy, dc)
            if h == 0 and phase == 0:
                pl.semaphore_wait(barrier, ND - 1)
                for k in range(1, NF):
                    pltpu.make_async_remote_copy(
                        src_ref=shsend, dst_ref=shrecv.at[frame], send_sem=sh_sem.at[0],
                        recv_sem=sh_sem.at[1], device_id=((frame + k) % NF, tile),
                        device_id_type=MESH).start()
            for dx, dz in INNER:
                for sign, (dy, dc) in zip((1, -1), pair):
                    ex, ez = (sign * dx) % NX, (sign * dz) % NZ
                    if (dy, dc, ex, ez) == (0, 0, 0, 0):
                        own[h].start()
                    else:
                        piece(h, phase, dy, dc, ex, ez).start()

    shrecv[frame] = shsend[...]
    for h in range(2):
        recv[h, :, 0] = jnp.zeros((NF, FP, CB, 128), jnp.bfloat16)
        recv[h, :, NT + 1] = jnp.zeros((NF, FP, CB, 128), jnp.bfloat16)

    offset = iota((F, F), 0) - iota((F, F), 1)
    for p in range(2):
        def put(i, acc):
            return jnp.where(offset == i, filters[p, i], acc)
        kmat[p] = lax.fori_loop(0, TAPS, put, jnp.zeros((F, F), jnp.float32)).astype(jnp.bfloat16)

    pltpu.make_async_copy(shrecv.at[pl.ds(0, NF - 1)], shrecv.at[pl.ds(0, NF - 1)], sh_sem.at[1]).wait()
    distance = iota((256, 128), 0) - ROWS - iota((256, 128), 1)

    def build(i, _):
        for q in range(2):
            shift = shrecv[i // FP, i % FP * 2 + q].astype(jnp.int32)
            bands[i, :, q * 128:(q + 1) * 128] = taps_of(distance + shift).astype(jnp.bfloat16)
        return 0

    lax.fori_loop(0, NF * FP, build, 0)

    load_weights.wait()

    def turn(i, _):
        p, j = i // 8, i % 8
        base = pl.multiple_of(i * 2048, 2048)
        for part in range(16):
            piece_w = wload[:, pl.ds(base + part * 128, 128)]
            tr[pl.ds(part * 128, 128), :] = piece_w.astype(jnp.float32).T
        for col in range(CB):
            got = tr[pl.ds(col, 128, stride=CB), :]
            wt[col // HC, j, p, pl.ds(col % HC * 128, 128), :] = got.astype(jnp.bfloat16)
        return 0

    lax.fori_loop(0, 16, turn, 0)

    row = iota((CB, 128), 1) % ROWS
    second = iota((CB, 128), 0) >= HC

    def vertical(h, source):
        def one(fp, _):
            shift = jnp.where(second, shrecv[source, 2 * fp + 1], shrecv[source, 2 * fp]).astype(jnp.int32) + row
            groups = []
            for b in range(4):
                tiles = []
                for j in range(8):
                    cell = recv[h, source, 2 * j + b, fp]
                    if 2 * j + b == 1:
                        cell = jnp.where(shift >= 0, cell.astype(jnp.float32), 0.0).astype(jnp.bfloat16)
                    if 2 * j + b == NT:
                        cell = jnp.where(shift < ROWS, cell.astype(jnp.float32), 0.0).astype(jnp.bfloat16)
                    tiles.append(cell)
                groups.append(jnp.concatenate(tiles, axis=0))
            lhs = jnp.concatenate([
                jnp.concatenate([groups[b][:, p * ROWS:(p + 1) * ROWS] for b in range(4)], axis=1)
                for p in range(2)], axis=0)
            res = jnp.dot(lhs, bands[source * FP + fp], preferred_element_type=jnp.float32) * UNSCALE
            res = res.reshape(CB, 2, HC, 256)
            for q in range(2):
                vbuf[pl.ds(source * FR + 2 * fp + q, 128, stride=F), :] = (
                    res[:, q, :, q * 128:(q + 1) * 128].reshape(128, 128))
            return 0

        lax.fori_loop(0, FP, one, 0, unroll=4)

    def pool(h):
        def one(j, acc):
            for p in range(2):
                cells = jnp.concatenate([
                    vbuf[pl.ds(pl.multiple_of(((p * 8 + j) * HC + c) * F, F), F), :].astype(jnp.bfloat16)
                    for c in range(HC)], axis=1)
                spikes = jnp.maximum(jnp.dot(kmat[p], cells, preferred_element_type=jnp.float32), 0.0)
                acc = acc + jnp.dot(spikes.astype(jnp.bfloat16), wt[h, j, p], preferred_element_type=jnp.float32)
            return acc
        return one

    acc = jnp.zeros((F, 128), jnp.float32)
    for h in range(2):
        for phase, pair in enumerate(PHASES):
            n = 31 if phase == NP - 1 else 32
            arrived = send.at[0, pl.ds(0, n)]
            pltpu.make_async_copy(arrived, arrived, recv_sem.at[h * NP + phase]).wait()
            if phase == NP - 1:
                own[h].wait()
            for dy, dc in pair:
                vertical(h, block_of(-dy, -dc))
        if h == 0:
            all_chips(idrecv, id_sem.at[1]).wait()
            own_id.wait()
            id_forward.start()
        acc = lax.fori_loop(0, 8, pool(h), acc, unroll=4)
        if h == 0:
            id_forward.wait_recv()
            got = jnp.concatenate([idrecv[core].reshape(NCHIP, 128), idsib[...].reshape(NCHIP, 128)], axis=0)
            component = iota((ND, COMP_DEV), 1).astype(jnp.float32)
            named = jnp.concatenate([(got[:, 0:COMP_DEV] == component).astype(jnp.float32),
                                     (got[:, 64:64 + COMP_DEV] == component).astype(jnp.float32)], axis=1).T
            for k in range(3):
                hot[:, k * 128:(k + 1) * 128] = named.astype(jnp.bfloat16)

    slots = lax.dot_general(sel[...], jnp.concatenate(three(acc), axis=1), (((1,), (1,)), ((), ())),
                            preferred_element_type=jnp.float32)
    fsend[...] = jnp.concatenate([slots[0:ND], slots[ND:]], axis=1).reshape(NC, NCHIP, 1, 128)
    chips(fsend, frecv, f_sem)
    own_f.start()

    for i in range(2 * NP):
        n = 31 if i % NP == NP - 1 else 32
        left = send.at[0, pl.ds(0, n)]
        pltpu.make_async_copy(left, left, send_sem.at[i]).wait()
    pltpu.make_async_copy(shrecv.at[pl.ds(0, NF - 1)], shrecv.at[pl.ds(0, NF - 1)], sh_sem.at[0]).wait()
    all_chips(idsend, id_sem.at[0]).wait()
    id_forward.wait_send()
    own_f.wait()
    all_chips(frecv, f_sem.at[1]).wait()
    forward.start()
    all_chips(fsend, f_sem.at[0]).wait()
    mine = frecv[core].reshape(NCHIP, 128)
    forward.wait_recv()
    rows = jnp.concatenate([mine, fsib[...].reshape(NCHIP, 128)], axis=0)
    total = jnp.dot(hot[...], jnp.concatenate(three(rows), axis=0), preferred_element_type=jnp.float32)
    out[...] = total[0:COMP_DEV, 0:F] + total[COMP_DEV:, F:2 * F]
    forward.wait_send()


def body(movie, shifts, filters, weights, slot_owner, slot_local):
    bf16, f32 = jnp.bfloat16, jnp.float32
    vmem = pl.BlockSpec(memory_space=pltpu.VMEM)
    smem = pl.BlockSpec(memory_space=pltpu.SMEM)
    anywhere = pl.BlockSpec(memory_space=pl.ANY)
    dma = pltpu.SemaphoreType.DMA
    return pl.pallas_call(
        kernel,
        out_shape=jax.ShapeDtypeStruct((COMP_DEV, F), f32),
        in_specs=[smem, smem, anywhere, anywhere, vmem, vmem],
        out_specs=vmem,
        scratch_shapes=[
            pltpu.VMEM((FR, 2, ROWS, W + 2 * PAD), bf16),
            pltpu.VMEM((FR, CB * NT, 512), bf16),
            pltpu.VMEM((2, ND, FP, CB, 128), bf16),
            pltpu.VMEM((2, NF, NT + 2, FP, CB, 128), bf16),
            pltpu.VMEM((FR, 1, 128), f32),
            pltpu.VMEM((NF, FR, 1, 128), f32),
            pltpu.VMEM((128, 32768), bf16),
            pltpu.VMEM((2048, 128), f32),
            pltpu.VMEM((2, 8, 2, HC * 128, 128), bf16),
            pltpu.VMEM((NF * FP, 256, 256), bf16),
            pltpu.VMEM((128 * F, 128), f32),
            pltpu.VMEM((2, F, F), bf16),
            pltpu.VMEM((2 * ND, 384), bf16),
            pltpu.VMEM((NC, NCHIP, 1, 128), f32),
            pltpu.VMEM((NC, NCHIP, 1, 128), f32),
            pltpu.VMEM((NCHIP, 1, 128), f32),
            pltpu.VMEM((2 * COMP_DEV, 384), bf16),
            pltpu.VMEM((NC, NCHIP, 1, 128), f32),
            pltpu.VMEM((NC, NCHIP, 1, 128), f32),
            pltpu.VMEM((NCHIP, 1, 128), f32),
            dma((2,)), dma((4,)), dma((2 * NP,)), dma((2 * NP,)), dma((2,)), dma((4,)), dma((4,)),
        ],
        compiler_params=pltpu.CompilerParams(
            collective_id=0, has_side_effects=True, vmem_limit_bytes=60 * 1024 * 1024),
        cost_estimate=pl.CostEstimate(flops=8_000_000_000, bytes_accessed=24_000_000, transcendentals=0),
    )(shifts.T, filters, movie, weights, slot_owner.reshape(1, -1), slot_local.reshape(1, -1))


def solution(mesh):
    in_specs = (
        P("frame", None, "tile", None),
        P("frame", None),
        P(),
        P(("frame", "tile"), None),
        P(("frame", "tile"), None),
        P(("frame", "tile"), None),
    )
    out_specs = P(("frame", "tile"), None)
    return jax.shard_map(body, mesh=mesh, in_specs=in_specs, out_specs=out_specs, check_vma=False)
```

```python
import jax
import jax.numpy as jnp
from jax import lax
from jax.experimental import pallas as pl
from jax.experimental.pallas import tpu as pltpu
from jax.sharding import PartitionSpec as P

COMP_DEV = 32
TAPS = 64
MAXS = 8
RAD = 3
CB = 16
MESH = pl.DeviceIdType.MESH

SCALE = 1.6543
TAP = (0.66015625, 0.400390625, 0.08935546875, 0.00732421875)
UNSCALE = 1.0 / (SCALE * SCALE)

NY, NC, NX, NZ = 4, 2, 4, 4
NF, NT, ND = 8, 16, 128
FR = 8
F = 64
ROWS = 64
W = 2048
PAD = 128

PHASES = (((1, 1), (3, 1)), ((1, 0), (3, 0)), ((0, 1), (2, 1)), ((2, 0), (0, 0)))
NP = len(PHASES)
GROUPS = tuple(group for pair in PHASES for group in pair)
NG = len(GROUPS)


def hops(*steps):
    return sum(min(v, 4 - v) for v in steps)


DIAGONAL = tuple((a, (a + b) % 4) for b in (2, 1, 3, 0) for a in (2, 1, 3, 0))
FAR = tuple(sorted(DIAGONAL, key=lambda d: -hops(*d)))
INNER = (DIAGONAL, DIAGONAL)
OTHERS = tuple(sorted(((dy, dc, dx, dz) for dx, dz in DIAGONAL for dy in (2, 1, 3, 0) for dc in (1, 0)
                       if (dy, dc, dx, dz) != (0, 0, 0, 0)), key=lambda d: -hops(d[0], d[2], d[3])))


def turns(pair, inner, apart):
    steps = [[(*group, sign * dx % NX, sign * dz % NZ) for dx, dz in inner] for sign, group in zip((1, -1), pair)]
    return steps[0] + steps[1] if apart else [step for both in zip(*steps) for step in both]


HC = CB // 2
FP = FR // 2


def taps_of(distance):
    d = jnp.abs(distance)
    out = jnp.where(d == 3, TAP[3], 0.0)
    out = jnp.where(d == 2, TAP[2], out)
    out = jnp.where(d == 1, TAP[1], out)
    return jnp.where(d == 0, TAP[0], out)


def three(value):
    high = value.astype(jnp.bfloat16)
    rest = value - high.astype(jnp.float32)
    middle = rest.astype(jnp.bfloat16)
    return [high, middle, (rest - middle.astype(jnp.float32)).astype(jnp.bfloat16)]


def iota(shape, dim):
    return lax.broadcasted_iota(jnp.int32, shape, dim)


def kernel(shifts, filters, movie, weights, owner, local, out,
           mbuf, smat, send, recv, shsend, shrecv, wload, tr, wt, bands, vbuf, kmat, sel,
           idsend, idrecv, hot, fsend, frecv,
           load_sem, own_sem, send_sem, recv_sem, sh_sem, id_sem, f_sem):
    frame = lax.axis_index("frame")
    tile = lax.axis_index("tile")
    y, core, x, z = frame // NC, frame % NC, tile // NZ, tile % NZ
    me = frame * NT + tile

    load_movie = pltpu.make_async_copy(movie, mbuf.at[:, :, :, pl.ds(PAD, W)], load_sem.at[0])
    load_movie.start()
    barrier = pltpu.get_barrier_semaphore()

    def block_of(dy, dc):
        return (y + dy) % NY * NC + (core + dc) % NC

    def tile_of(dx, dz):
        return (x + dx) % NX * NZ + (z + dz) % NZ

    for dy, dc, dx, dz in OTHERS:
        pl.semaphore_signal(barrier, inc=1, device_id=(block_of(dy, dc), tile_of(dx, dz)), device_id_type=MESH)

    line = iota((128, 384), 0)
    place = line % 64 // HC * CB + line // 64 * HC + line % HC
    across = iota((128, 384), 1) - PAD - place
    for f in range(FR):
        stencil = taps_of(across + shifts[1, f]).astype(jnp.bfloat16)
        for h in range(2):
            for a in range(2):
                r = h * 128 + a * 64
                smat[f, r:r + 64, a * 128:a * 128 + 384] = stencil[h * 64:h * 64 + 64]
                blank = 384 - a * 384
                smat[f, r:r + 64, blank:blank + 128] = jnp.zeros((64, 128), jnp.bfloat16)
        shsend[f] = jnp.full((1, 128), shifts[0, f], jnp.int32).astype(jnp.float32)
    mbuf[:, :, :, 0:PAD] = jnp.zeros((FR, 2, ROWS, PAD), jnp.bfloat16)
    mbuf[:, :, :, PAD + W:] = jnp.zeros((FR, 2, ROWS, PAD), jnp.bfloat16)
    load_movie.wait()
    load_weights = pltpu.make_async_copy(weights, wload, load_sem.at[1])
    load_weights.start()
    lane = iota((2, ROWS, PAD), 2)
    for f in range(FR):
        s = shifts[1, f]
        first = mbuf[f, :, :, PAD:2 * PAD].astype(jnp.float32)
        mbuf[f, :, :, PAD:2 * PAD] = jnp.where(lane + s >= 0, first, 0.0).astype(jnp.bfloat16)
        last = mbuf[f, :, :, W:W + PAD].astype(jnp.float32)
        mbuf[f, :, :, W:W + PAD] = jnp.where(lane + s < PAD, last, 0.0).astype(jnp.bfloat16)

    def smooth_block(dy, dc):
        block = block_of(dy, dc)

        def one(fp, _):
            res = []
            for q in range(2):
                f = 2 * fp + q
                window = mbuf[f, :, :, pl.ds(pl.multiple_of(block * CB * NT, CB * NT), 512)]
                cols = lax.dot_general(smat[f], window.reshape(2 * ROWS, 512), (((1,), (1,)), ((), ())),
                                       preferred_element_type=jnp.float32)
                res.append(cols.reshape(2 * NT, HC, 128))
            both = jnp.concatenate(res, axis=1).astype(jnp.bfloat16)
            for h in range(2):
                send[h, pl.ds(block * NT, NT), fp] = both[h * NT:(h + 1) * NT]
            return 0

        lax.fori_loop(0, FP, one, 0, unroll=2)

    def piece(h, dy, dc, dx, dz):
        group = h * NG + GROUPS.index((dy, dc))
        b, t = block_of(dy, dc), tile_of(dx, dz)
        return pltpu.make_async_remote_copy(
            src_ref=send.at[h, b * NT + t], dst_ref=recv.at[h, frame, tile + 1],
            send_sem=send_sem.at[group], recv_sem=recv_sem.at[group],
            device_id=(b, t), device_id_type=MESH)

    def rows_out(src, dst, sems):
        for dy, dc, dx, dz in OTHERS:
            b, t = block_of(dy, dc), tile_of(dx, dz)
            pltpu.make_async_remote_copy(
                src_ref=src.at[pl.ds(b * NT + t, 1)], dst_ref=dst.at[pl.ds(me, 1)], send_sem=sems.at[0],
                recv_sem=sems.at[1], device_id=(b, t), device_id_type=MESH).start()

    def all_rows(ref, sem):
        part = ref.at[pl.ds(0, ND - 1)]
        return pltpu.make_async_copy(part, part, sem)

    def name_entries():
        owns = (owner[...] == iota((ND, 128), 0)).astype(jnp.float32)
        before = (iota((128, 128), 0) < iota((128, 128), 1)).astype(jnp.bfloat16)
        count = jnp.dot(owns.astype(jnp.bfloat16), before, preferred_element_type=jnp.float32)
        ids = local[...].astype(jnp.float32)
        names = []
        for slot in range(2):
            taken = jnp.where(count == float(slot), owns, 0.0)
            for k in range(3):
                sel[slot * ND:(slot + 1) * ND, k * 128:(k + 1) * 128] = taken.astype(jnp.bfloat16)
            names.append(jnp.broadcast_to(jnp.sum(taken * ids, axis=1, keepdims=True), (ND, 64)))
        idsend[...] = jnp.concatenate(names, axis=1)
        rows_out(idsend, idrecv, id_sem)
        own_id.start()

    own_id = pltpu.make_async_copy(idsend.at[pl.ds(me, 1)], idrecv.at[pl.ds(me, 1)], own_sem.at[2])
    own_f = pltpu.make_async_copy(fsend.at[pl.ds(me, 1)], frecv.at[pl.ds(me, 1)], own_sem.at[3])

    own = [pltpu.make_async_copy(send.at[h, me], recv.at[h, frame, tile + 1], own_sem.at[h]) for h in range(2)]
    for h in range(2):
        if h == 1:
            name_entries()
        for phase, pair in enumerate(PHASES):
            if h == 0:
                for dy, dc in pair:
                    smooth_block(dy, dc)
            if h == 0 and phase == 0:
                pl.semaphore_wait(barrier, ND - 1)
                for k in range(1, NF):
                    pltpu.make_async_remote_copy(
                        src_ref=shsend, dst_ref=shrecv.at[frame], send_sem=sh_sem.at[0],
                        recv_sem=sh_sem.at[1], device_id=((frame + k) % NF, tile),
                        device_id_type=MESH).start()
            last = h == 1 and phase == NP - 1
            for step in turns(pair, FAR if last else INNER[h], last):
                if step == (0, 0, 0, 0):
                    own[h].start()
                else:
                    piece(h, *step).start()

    shrecv[frame] = shsend[...]
    for h in range(2):
        recv[h, :, 0] = jnp.zeros((NF, FP, CB, 128), jnp.bfloat16)
        recv[h, :, NT + 1] = jnp.zeros((NF, FP, CB, 128), jnp.bfloat16)

    offset = iota((F, F), 0) - iota((F, F), 1)
    for p in range(2):
        def put(i, acc):
            return jnp.where(offset == i, filters[p, i], acc)
        kmat[p] = lax.fori_loop(0, TAPS, put, jnp.zeros((F, F), jnp.float32)).astype(jnp.bfloat16)

    pltpu.make_async_copy(shrecv.at[pl.ds(0, NF - 1)], shrecv.at[pl.ds(0, NF - 1)], sh_sem.at[1]).wait()
    distance = iota((256, 128), 0) - ROWS - iota((256, 128), 1)

    def build(i, _):
        for q in range(2):
            shift = shrecv[i // FP, i % FP * 2 + q].astype(jnp.int32)
            bands[i, :, q * 128:(q + 1) * 128] = taps_of(distance + shift).astype(jnp.bfloat16)
        return 0

    lax.fori_loop(0, NF * FP, build, 0)

    load_weights.wait()

    def turn(i, _):
        p, j = i // 8, i % 8
        base = pl.multiple_of(i * 2048, 2048)
        for part in range(16):
            piece_w = wload[:, pl.ds(base + part * 128, 128)]
            tr[pl.ds(part * 128, 128), :] = piece_w.astype(jnp.float32).T
        for col in range(CB):
            got = tr[pl.ds(col, 128, stride=CB), :]
            wt[col // HC, j, p, pl.ds(col % HC * 128, 128), :] = got.astype(jnp.bfloat16)
        return 0

    lax.fori_loop(0, 16, turn, 0)

    row = iota((CB, 128), 1) % ROWS
    second = iota((CB, 128), 0) >= HC

    def pieces(g, sem):
        part = send.at[0, pl.ds(0, NT - (GROUPS[g] == (0, 0)))]
        return pltpu.make_async_copy(part, part, sem)

    def vertical(h, source):
        def one(fp, _):
            shift = jnp.where(second, shrecv[source, 2 * fp + 1], shrecv[source, 2 * fp]).astype(jnp.int32) + row
            groups = []
            for b in range(4):
                tiles = []
                for j in range(8):
                    cell = recv[h, source, 2 * j + b, fp]
                    if 2 * j + b == 1:
                        cell = jnp.where(shift >= 0, cell.astype(jnp.float32), 0.0).astype(jnp.bfloat16)
                    if 2 * j + b == NT:
                        cell = jnp.where(shift < ROWS, cell.astype(jnp.float32), 0.0).astype(jnp.bfloat16)
                    tiles.append(cell)
                groups.append(jnp.concatenate(tiles, axis=0))
            lhs = jnp.concatenate([
                jnp.concatenate([groups[b][:, p * ROWS:(p + 1) * ROWS] for b in range(4)], axis=1)
                for p in range(2)], axis=0)
            res = jnp.dot(lhs, bands[source * FP + fp], preferred_element_type=jnp.float32) * UNSCALE
            res = res.reshape(CB, 2, HC, 256)
            for q in range(2):
                vbuf[pl.ds(source * FR + 2 * fp + q, 128, stride=F), :] = (
                    res[:, q, :, q * 128:(q + 1) * 128].reshape(128, 128))
            return 0

        lax.fori_loop(0, FP, one, 0, unroll=4)

    def pool(h):
        def one(j, acc):
            both = []
            for p in range(2):
                cells = jnp.concatenate([
                    vbuf[pl.ds(pl.multiple_of(((p * 8 + j) * HC + c) * F, F), F), :].astype(jnp.bfloat16)
                    for c in range(HC)], axis=1)
                spikes = jnp.maximum(jnp.dot(kmat[p], cells, preferred_element_type=jnp.float32), 0.0)
                both.append(spikes.astype(jnp.bfloat16))
            return acc + jnp.dot(jnp.concatenate(both, axis=1), wt[h, j].reshape(2 * HC * 128, 128),
                                 preferred_element_type=jnp.float32)
        return one

    acc = jnp.zeros((F, 128), jnp.float32)
    for h in range(2):
        for g, (dy, dc) in enumerate(GROUPS):
            pieces(g, recv_sem.at[h * NG + g]).wait()
            if (dy, dc) == (0, 0):
                own[h].wait()
            vertical(h, block_of(-dy, -dc))
        acc = lax.fori_loop(0, 8, pool(h), acc, unroll=4)
        if h == 0:
            all_rows(idrecv, id_sem.at[1]).wait()
            own_id.wait()
            got = idrecv[...]
            component = iota((ND, COMP_DEV), 1).astype(jnp.float32)
            named = jnp.concatenate([(got[:, 0:COMP_DEV] == component).astype(jnp.float32),
                                     (got[:, 64:64 + COMP_DEV] == component).astype(jnp.float32)], axis=1).T
            for k in range(3):
                hot[:, k * 128:(k + 1) * 128] = named.astype(jnp.bfloat16)

    slots = lax.dot_general(sel[...], jnp.concatenate(three(acc), axis=1), (((1,), (1,)), ((), ())),
                            preferred_element_type=jnp.float32)
    fsend[...] = jnp.concatenate([slots[0:ND], slots[ND:]], axis=1)
    rows_out(fsend, frecv, f_sem)
    own_f.start()

    for i in range(2 * NG):
        pieces(i % NG, send_sem.at[i]).wait()
    pltpu.make_async_copy(shrecv.at[pl.ds(0, NF - 1)], shrecv.at[pl.ds(0, NF - 1)], sh_sem.at[0]).wait()
    all_rows(idsend, id_sem.at[0]).wait()
    own_f.wait()
    all_rows(fsend, f_sem.at[0]).wait()
    all_rows(frecv, f_sem.at[1]).wait()
    rows = frecv[...]
    total = jnp.dot(hot[...], jnp.concatenate(three(rows), axis=0), preferred_element_type=jnp.float32)
    out[...] = total[0:COMP_DEV, 0:F] + total[COMP_DEV:, F:2 * F]


def body(movie, shifts, filters, weights, slot_owner, slot_local):
    bf16, f32 = jnp.bfloat16, jnp.float32
    vmem = pl.BlockSpec(memory_space=pltpu.VMEM)
    smem = pl.BlockSpec(memory_space=pltpu.SMEM)
    anywhere = pl.BlockSpec(memory_space=pl.ANY)
    dma = pltpu.SemaphoreType.DMA
    return pl.pallas_call(
        kernel,
        out_shape=jax.ShapeDtypeStruct((COMP_DEV, F), f32),
        in_specs=[smem, smem, anywhere, anywhere, vmem, vmem],
        out_specs=vmem,
        scratch_shapes=[
            pltpu.VMEM((FR, 2, ROWS, W + 2 * PAD), bf16),
            pltpu.VMEM((FR, CB * NT, 512), bf16),
            pltpu.VMEM((2, ND, FP, CB, 128), bf16),
            pltpu.VMEM((2, NF, NT + 2, FP, CB, 128), bf16),
            pltpu.VMEM((FR, 1, 128), f32),
            pltpu.VMEM((NF, FR, 1, 128), f32),
            pltpu.VMEM((128, 32768), bf16),
            pltpu.VMEM((2048, 128), f32),
            pltpu.VMEM((2, 8, 2, HC * 128, 128), bf16),
            pltpu.VMEM((NF * FP, 256, 256), bf16),
            pltpu.VMEM((128 * F, 128), f32),
            pltpu.VMEM((2, F, F), bf16),
            pltpu.VMEM((2 * ND, 384), bf16),
            pltpu.VMEM((ND, 128), f32),
            pltpu.VMEM((ND, 128), f32),
            pltpu.VMEM((2 * COMP_DEV, 384), bf16),
            pltpu.VMEM((ND, 128), f32),
            pltpu.VMEM((ND, 128), f32),
            dma((2,)), dma((4,)), dma((2 * NG,)), dma((2 * NG,)), dma((2,)), dma((2,)), dma((2,)),
        ],
        compiler_params=pltpu.CompilerParams(
            collective_id=0, has_side_effects=True, vmem_limit_bytes=60 * 1024 * 1024),
        cost_estimate=pl.CostEstimate(flops=8_000_000_000, bytes_accessed=24_000_000, transcendentals=0),
    )(shifts.T, filters, movie, weights, slot_owner.reshape(1, -1), slot_local.reshape(1, -1))


def solution(mesh):
    in_specs = (
        P("frame", None, "tile", None),
        P("frame", None),
        P(),
        P(("frame", "tile"), None),
        P(("frame", "tile"), None),
        P(("frame", "tile"), None),
    )
    out_specs = P(("frame", "tile"), None)
    return jax.shard_map(body, mesh=mesh, in_specs=in_specs, out_specs=out_specs, check_vma=False)
```

```python
import jax
import jax.numpy as jnp
from jax import lax
from jax.experimental import pallas as pl
from jax.experimental.pallas import tpu as pltpu
from jax.sharding import PartitionSpec as P

COMP_DEV = 32
TAPS = 64
MAXS = 8
RAD = 3
CB = 16
MESH = pl.DeviceIdType.MESH

SCALE = 1.6543
TAP = (0.66015625, 0.400390625, 0.08935546875, 0.00732421875)
UNSCALE = 1.0 / (SCALE * SCALE)

NY, NC, NX, NZ = 4, 2, 4, 4
NF, NT, ND = 8, 16, 128
FR = 8
F = 64
ROWS = 64
W = 2048
PAD = 128

PHASES = (((1, 1), (3, 1)), ((1, 0), (3, 0)), ((0, 1), (2, 1)), ((2, 0), (0, 0)))
NP = len(PHASES)
GROUPS = tuple(group for pair in PHASES for group in pair)
NG = len(GROUPS)


def hops(*steps):
    return sum(min(v, 4 - v) for v in steps)


DIAGONAL = tuple((a, (a + b) % 4) for b in (2, 1, 3, 0) for a in (2, 1, 3, 0))
FAR = tuple(sorted(DIAGONAL, key=lambda d: -hops(*d)))
INNER = (DIAGONAL, DIAGONAL)
OTHERS = tuple(sorted(((dy, dc, dx, dz) for dx, dz in DIAGONAL for dy in (2, 1, 3, 0) for dc in (1, 0)
                       if (dy, dc, dx, dz) != (0, 0, 0, 0)), key=lambda d: -hops(d[0], d[2], d[3])))


def turns(pair, inner, apart):
    steps = [[(*group, sign * dx % NX, sign * dz % NZ) for dx, dz in inner] for sign, group in zip((1, -1), pair)]
    return steps[0] + steps[1] if apart else [step for both in zip(*steps) for step in both]


HC = CB // 2
FP = FR // 2


def taps_of(distance):
    d = jnp.abs(distance)
    out = jnp.where(d == 3, TAP[3], 0.0)
    out = jnp.where(d == 2, TAP[2], out)
    out = jnp.where(d == 1, TAP[1], out)
    return jnp.where(d == 0, TAP[0], out)


def three(value):
    high = value.astype(jnp.bfloat16)
    rest = value - high.astype(jnp.float32)
    middle = rest.astype(jnp.bfloat16)
    return [high, middle, (rest - middle.astype(jnp.float32)).astype(jnp.bfloat16)]


def iota(shape, dim):
    return lax.broadcasted_iota(jnp.int32, shape, dim)


def kernel(shifts, filters, movie, weights, owner, local, out,
           mbuf, smat, send, recv, shsend, shrecv, wload, tr, wt, bands, vbuf, kmat, sel,
           idsend, idrecv, hot, fsend, frecv,
           load_sem, own_sem, send_sem, recv_sem, sh_sem, id_sem, f_sem):
    frame = lax.axis_index("frame")
    tile = lax.axis_index("tile")
    y, core, x, z = frame // NC, frame % NC, tile // NZ, tile % NZ
    me = frame * NT + tile

    load_movie = pltpu.make_async_copy(movie, mbuf.at[:, :, :, pl.ds(PAD, W)], load_sem.at[0])
    load_movie.start()
    barrier = pltpu.get_barrier_semaphore()

    def block_of(dy, dc):
        return (y + dy) % NY * NC + (core + dc) % NC

    def tile_of(dx, dz):
        return (x + dx) % NX * NZ + (z + dz) % NZ

    for dy, dc, dx, dz in OTHERS:
        pl.semaphore_signal(barrier, inc=1, device_id=(block_of(dy, dc), tile_of(dx, dz)), device_id_type=MESH)

    line = iota((128, 384), 0)
    place = line % 64 // HC * CB + line // 64 * HC + line % HC
    across = iota((128, 384), 1) - PAD - place
    for f in range(FR):
        stencil = taps_of(across + shifts[1, f]).astype(jnp.bfloat16)
        for h in range(2):
            for a in range(2):
                r = h * 128 + a * 64
                smat[f, r:r + 64, a * 128:a * 128 + 384] = stencil[h * 64:h * 64 + 64]
                blank = 384 - a * 384
                smat[f, r:r + 64, blank:blank + 128] = jnp.zeros((64, 128), jnp.bfloat16)
        shsend[f] = jnp.full((1, 128), shifts[0, f], jnp.int32).astype(jnp.float32)
    mbuf[:, :, :, 0:PAD] = jnp.zeros((FR, 2, ROWS, PAD), jnp.bfloat16)
    mbuf[:, :, :, PAD + W:] = jnp.zeros((FR, 2, ROWS, PAD), jnp.bfloat16)
    load_movie.wait()
    load_weights = pltpu.make_async_copy(weights, wload, load_sem.at[1])
    load_weights.start()
    lane = iota((2, ROWS, PAD), 2)
    for f in range(FR):
        s = shifts[1, f]
        first = mbuf[f, :, :, PAD:2 * PAD].astype(jnp.float32)
        mbuf[f, :, :, PAD:2 * PAD] = jnp.where(lane + s >= 0, first, 0.0).astype(jnp.bfloat16)
        last = mbuf[f, :, :, W:W + PAD].astype(jnp.float32)
        mbuf[f, :, :, W:W + PAD] = jnp.where(lane + s < PAD, last, 0.0).astype(jnp.bfloat16)

    def smooth_block(dy, dc):
        block = block_of(dy, dc)

        def one(fp, _):
            res = []
            for q in range(2):
                f = 2 * fp + q
                window = mbuf[f, :, :, pl.ds(pl.multiple_of(block * CB * NT, CB * NT), 512)]
                cols = lax.dot_general(smat[f], window.reshape(2 * ROWS, 512), (((1,), (1,)), ((), ())),
                                       preferred_element_type=jnp.float32)
                res.append(cols.reshape(2 * NT, HC, 128))
            both = jnp.concatenate(res, axis=1).astype(jnp.bfloat16)
            for h in range(2):
                send[h, pl.ds(block * NT, NT), fp] = both[h * NT:(h + 1) * NT]
            return 0

        lax.fori_loop(0, FP, one, 0, unroll=2)

    def piece(h, dy, dc, dx, dz):
        group = h * NG + GROUPS.index((dy, dc))
        b, t = block_of(dy, dc), tile_of(dx, dz)
        return pltpu.make_async_remote_copy(
            src_ref=send.at[h, b * NT + t], dst_ref=recv.at[h, frame, tile + 1],
            send_sem=send_sem.at[group], recv_sem=recv_sem.at[group],
            device_id=(b, t), device_id_type=MESH)

    def rows_out(src, dst, sems):
        for dy, dc, dx, dz in OTHERS:
            b, t = block_of(dy, dc), tile_of(dx, dz)
            pltpu.make_async_remote_copy(
                src_ref=src.at[pl.ds(b * NT + t, 1)], dst_ref=dst.at[pl.ds(me, 1)], send_sem=sems.at[0],
                recv_sem=sems.at[1], device_id=(b, t), device_id_type=MESH).start()

    def all_rows(ref, sem):
        part = ref.at[pl.ds(0, ND - 1)]
        return pltpu.make_async_copy(part, part, sem)

    def name_entries():
        owns = (owner[...] == iota((ND, 128), 0)).astype(jnp.float32)
        before = (iota((128, 128), 0) < iota((128, 128), 1)).astype(jnp.bfloat16)
        count = jnp.dot(owns.astype(jnp.bfloat16), before, preferred_element_type=jnp.float32)
        ids = local[...].astype(jnp.float32)
        names = []
        for slot in range(2):
            taken = jnp.where(count == float(slot), owns, 0.0)
            for k in range(3):
                sel[slot * ND:(slot + 1) * ND, k * 128:(k + 1) * 128] = taken.astype(jnp.bfloat16)
            names.append(jnp.broadcast_to(jnp.sum(taken * ids, axis=1, keepdims=True), (ND, 64)))
        idsend[...] = jnp.concatenate(names, axis=1)
        rows_out(idsend, idrecv, id_sem)
        own_id.start()

    own_id = pltpu.make_async_copy(idsend.at[pl.ds(me, 1)], idrecv.at[pl.ds(me, 1)], own_sem.at[2])
    own_f = pltpu.make_async_copy(fsend.at[pl.ds(me, 1)], frecv.at[pl.ds(me, 1)], own_sem.at[3])

    own = [pltpu.make_async_copy(send.at[h, me], recv.at[h, frame, tile + 1], own_sem.at[h]) for h in range(2)]
    for h in range(2):
        if h == 1:
            name_entries()
        for phase, pair in enumerate(PHASES):
            if h == 0:
                for dy, dc in pair:
                    smooth_block(dy, dc)
            if h == 0 and phase == 0:
                pl.semaphore_wait(barrier, ND - 1)
            last = h == 1 and phase == NP - 1
            for step in turns(pair, FAR if last else INNER[h], last):
                if step == (0, 0, 0, 0):
                    own[h].start()
                else:
                    piece(h, *step).start()
            if h == 0 and phase == 0:
                for k in range(1, NF):
                    pltpu.make_async_remote_copy(
                        src_ref=shsend, dst_ref=shrecv.at[frame], send_sem=sh_sem.at[0],
                        recv_sem=sh_sem.at[1], device_id=((frame + k) % NF, tile),
                        device_id_type=MESH).start()

    shrecv[frame] = shsend[...]
    for h in range(2):
        recv[h, :, 0] = jnp.zeros((NF, FP, CB, 128), jnp.bfloat16)
        recv[h, :, NT + 1] = jnp.zeros((NF, FP, CB, 128), jnp.bfloat16)

    offset = iota((F, F), 0) - iota((F, F), 1)
    for p in range(2):
        def put(i, acc):
            return jnp.where(offset == i, filters[p, i], acc)
        kmat[p] = lax.fori_loop(0, TAPS, put, jnp.zeros((F, F), jnp.float32)).astype(jnp.bfloat16)

    pltpu.make_async_copy(shrecv.at[pl.ds(0, NF - 1)], shrecv.at[pl.ds(0, NF - 1)], sh_sem.at[1]).wait()
    distance = iota((256, 128), 0) - ROWS - iota((256, 128), 1)

    def build(i, _):
        for q in range(2):
            shift = shrecv[i // FP, i % FP * 2 + q].astype(jnp.int32)
            bands[i, :, q * 128:(q + 1) * 128] = taps_of(distance + shift).astype(jnp.bfloat16)
        return 0

    lax.fori_loop(0, NF * FP, build, 0)

    load_weights.wait()

    def turn(i, _):
        p, j = i // 8, i % 8
        base = pl.multiple_of(i * 2048, 2048)
        for part in range(16):
            piece_w = wload[:, pl.ds(base + part * 128, 128)]
            tr[pl.ds(part * 128, 128), :] = piece_w.astype(jnp.float32).T
        for col in range(CB):
            got = tr[pl.ds(col, 128, stride=CB), :]
            wt[col // HC, j, p, pl.ds(col % HC * 128, 128), :] = got.astype(jnp.bfloat16)
        return 0

    lax.fori_loop(0, 16, turn, 0)

    row = iota((CB, 128), 1) % ROWS
    second = iota((CB, 128), 0) >= HC

    def pieces(g, sem):
        part = send.at[0, pl.ds(0, NT - (GROUPS[g] == (0, 0)))]
        return pltpu.make_async_copy(part, part, sem)

    def vertical(h, source):
        def one(fp, _):
            shift = jnp.where(second, shrecv[source, 2 * fp + 1], shrecv[source, 2 * fp]).astype(jnp.int32) + row
            groups = []
            for b in range(4):
                tiles = []
                for j in range(8):
                    cell = recv[h, source, 2 * j + b, fp]
                    if 2 * j + b == 1:
                        cell = jnp.where(shift >= 0, cell.astype(jnp.float32), 0.0).astype(jnp.bfloat16)
                    if 2 * j + b == NT:
                        cell = jnp.where(shift < ROWS, cell.astype(jnp.float32), 0.0).astype(jnp.bfloat16)
                    tiles.append(cell)
                groups.append(jnp.concatenate(tiles, axis=0))
            lhs = jnp.concatenate([
                jnp.concatenate([groups[b][:, p * ROWS:(p + 1) * ROWS] for b in range(4)], axis=1)
                for p in range(2)], axis=0)
            res = jnp.dot(lhs, bands[source * FP + fp], preferred_element_type=jnp.float32) * UNSCALE
            res = res.reshape(CB, 2, HC, 256)
            for q in range(2):
                vbuf[pl.ds(source * FR + 2 * fp + q, 128, stride=F), :] = (
                    res[:, q, :, q * 128:(q + 1) * 128].reshape(128, 128))
            return 0

        lax.fori_loop(0, FP, one, 0, unroll=4)

    def pool(h):
        def one(j, acc):
            both = []
            for p in range(2):
                cells = jnp.concatenate([
                    vbuf[pl.ds(pl.multiple_of(((p * 8 + j) * HC + c) * F, F), F), :].astype(jnp.bfloat16)
                    for c in range(HC)], axis=1)
                spikes = jnp.maximum(jnp.dot(kmat[p], cells, preferred_element_type=jnp.float32), 0.0)
                both.append(spikes.astype(jnp.bfloat16))
            return acc + jnp.dot(jnp.concatenate(both, axis=1), wt[h, j].reshape(2 * HC * 128, 128),
                                 preferred_element_type=jnp.float32)
        return one

    acc = jnp.zeros((F, 128), jnp.float32)
    for h in range(2):
        for g, (dy, dc) in enumerate(GROUPS):
            pieces(g, recv_sem.at[h * NG + g]).wait()
            if (dy, dc) == (0, 0):
                own[h].wait()
            vertical(h, block_of(-dy, -dc))
        acc = lax.fori_loop(0, 8, pool(h), acc, unroll=8)
        if h == 0:
            all_rows(idrecv, id_sem.at[1]).wait()
            own_id.wait()
            got = idrecv[...]
            component = iota((ND, COMP_DEV), 1).astype(jnp.float32)
            named = jnp.concatenate([(got[:, 0:COMP_DEV] == component).astype(jnp.float32),
                                     (got[:, 64:64 + COMP_DEV] == component).astype(jnp.float32)], axis=1).T
            for k in range(3):
                hot[:, k * 128:(k + 1) * 128] = named.astype(jnp.bfloat16)

    slots = lax.dot_general(sel[...], jnp.concatenate(three(acc), axis=1), (((1,), (1,)), ((), ())),
                            preferred_element_type=jnp.float32)
    fsend[...] = jnp.concatenate([slots[0:ND], slots[ND:]], axis=1)
    rows_out(fsend, frecv, f_sem)
    own_f.start()

    for i in range(2 * NG):
        pieces(i % NG, send_sem.at[i]).wait()
    pltpu.make_async_copy(shrecv.at[pl.ds(0, NF - 1)], shrecv.at[pl.ds(0, NF - 1)], sh_sem.at[0]).wait()
    all_rows(idsend, id_sem.at[0]).wait()
    own_f.wait()
    all_rows(fsend, f_sem.at[0]).wait()
    all_rows(frecv, f_sem.at[1]).wait()
    rows = frecv[...]
    total = jnp.dot(hot[...], jnp.concatenate(three(rows), axis=0), preferred_element_type=jnp.float32)
    out[...] = total[0:COMP_DEV, 0:F] + total[COMP_DEV:, F:2 * F]


def body(movie, shifts, filters, weights, slot_owner, slot_local):
    bf16, f32 = jnp.bfloat16, jnp.float32
    vmem = pl.BlockSpec(memory_space=pltpu.VMEM)
    smem = pl.BlockSpec(memory_space=pltpu.SMEM)
    anywhere = pl.BlockSpec(memory_space=pl.ANY)
    dma = pltpu.SemaphoreType.DMA
    return pl.pallas_call(
        kernel,
        out_shape=jax.ShapeDtypeStruct((COMP_DEV, F), f32),
        in_specs=[smem, smem, anywhere, anywhere, vmem, vmem],
        out_specs=vmem,
        scratch_shapes=[
            pltpu.VMEM((FR, 2, ROWS, W + 2 * PAD), bf16),
            pltpu.VMEM((FR, CB * NT, 512), bf16),
            pltpu.VMEM((2, ND, FP, CB, 128), bf16),
            pltpu.VMEM((2, NF, NT + 2, FP, CB, 128), bf16),
            pltpu.VMEM((FR, 1, 128), f32),
            pltpu.VMEM((NF, FR, 1, 128), f32),
            pltpu.VMEM((128, 32768), bf16),
            pltpu.VMEM((2048, 128), f32),
            pltpu.VMEM((2, 8, 2, HC * 128, 128), bf16),
            pltpu.VMEM((NF * FP, 256, 256), bf16),
            pltpu.VMEM((128 * F, 128), f32),
            pltpu.VMEM((2, F, F), bf16),
            pltpu.VMEM((2 * ND, 384), bf16),
            pltpu.VMEM((ND, 128), f32),
            pltpu.VMEM((ND, 128), f32),
            pltpu.VMEM((2 * COMP_DEV, 384), bf16),
            pltpu.VMEM((ND, 128), f32),
            pltpu.VMEM((ND, 128), f32),
            dma((2,)), dma((4,)), dma((2 * NG,)), dma((2 * NG,)), dma((2,)), dma((2,)), dma((2,)),
        ],
        compiler_params=pltpu.CompilerParams(
            collective_id=0, has_side_effects=True, vmem_limit_bytes=60 * 1024 * 1024),
        cost_estimate=pl.CostEstimate(flops=8_000_000_000, bytes_accessed=24_000_000, transcendentals=0),
    )(shifts.T, filters, movie, weights, slot_owner.reshape(1, -1), slot_local.reshape(1, -1))


def solution(mesh):
    in_specs = (
        P("frame", None, "tile", None),
        P("frame", None),
        P(),
        P(("frame", "tile"), None),
        P(("frame", "tile"), None),
        P(("frame", "tile"), None),
    )
    out_specs = P(("frame", "tile"), None)
    return jax.shard_map(body, mesh=mesh, in_specs=in_specs, out_specs=out_specs, check_vma=False)
```
